32 devices in a mesh: dp: 8 (over z, y), shard: 4 (over x, core).
Axes of the slice: x: 2, y: 2, z: 4, core: 2. Of those that a mesh axis runs over, the one named last changes fastest.
Arguments:
- embedded: bfloat16 [30720, 1280], P(('dp', 'shard')), may hold values from -6 to 6
- mask_token_embedding: bfloat16 [1280], replicated, may hold values from -5 to 5
- destination: int32 [30720], P(('dp', 'shard')), may hold values from 0 to 8, as said below
- position: int32 [30720], P(('dp', 'shard')), may hold values from 0 to 79, as said below
- length: int32 [30720], P(('dp', 'shard')), may hold values from 0 to 80, as said below
- unmask_order: int32 [30720], P(('dp', 'shard')), may hold values from 0 to 79, as said below
- timestep: int32 [30720], P(('dp', 'shard')), may hold values from 0 to 80, as said below
- upstream: bfloat16 [12288, 1280], P(('dp', 'shard')), may hold values from -0.29882812 to 0.29882812
- gain_in: float32 [1280], replicated, may hold values from 0.4 to 1.6
- weight_in: bfloat16 [1280, 640], replicated, may hold values from -0.15625 to 0.15625
- gain_mid: float32 [640], replicated, may hold values from 0.4 to 1.6
- weight_conv: bfloat16 [640, 5, 640], replicated, may hold values from -0.109375 to 0.109375
- gain_out: float32 [640], replicated, may hold values from 0.4 to 1.6
- weight_out: bfloat16 [1280, 640], replicated, may hold values from -0.25 to 0.25
Outputs:
- grad_input: bfloat16 [12288, 1280], P(('dp', 'shard'))
- grad_weight_in: float32 [1280, 640], P('dp', 'shard')
- grad_weight_conv: float32 [640, 5, 640], P('dp', None, 'shard')
- grad_weight_out: float32 [1280, 640], P('dp', 'shard')
The draws below stay inside these ranges and needn't reach their ends.
Inputs may be any that keep to these rules, and one draw needn't show every extreme that they name: 8 marks an empty slot. All slots of a sequence share one destination. Among the devices of one shard index, every destination receives exactly 384 rows, and one device sends one destination at most one sequence. A device's slots hold whole sequences one after another from its first slot, each in order of position; empty slots come last and hold 0. `length`: 0 on empty slots; equal on all slots of a sequence; every destination receives one sequence of exactly 80 residues. `unmask_order`: within each sequence a permutation of its positions; 0 on empty slots. `timestep`: equal on all slots of a sequence, from 1 to its length; 0 on empty slots.
All inputs are finite; a program needn't handle non-finite values.
Results may differ from the reference program's by a relative error of at most 0.0074.
Values may be sent and summed in bfloat16 or wider, within the bound.
A program may use at most 192 MiB of HBM per device.

```python
import jax
import jax.numpy as jnp
from jax import lax

D = 1280
H = 640
KERNEL_TAPS = 5
DILATION_STEP = 16
LMAX = 80
SEQ_OWN = 6
TOK = 384
LSLOT = 960
OWN_ROWS = 12288
LOAD_ROWS = 30720
N_DP = 8
N_SHARD = 4


def build_layout(key):
    key = jax.random.fold_in(key, 4242)
    key_start, key_size, key_rank, key_time = jax.random.split(key, 4)
    owner_ids = jnp.arange(N_DP, dtype=jnp.int32)
    piece_ids = jnp.arange(SEQ_OWN, dtype=jnp.int32)
    spread = jax.random.randint(key_size, (N_SHARD, N_DP, SEQ_OWN // 2), 0, 17, dtype=jnp.int32)
    spread = spread.at[:, :, 0].set(16)
    piece_sizes = jnp.stack([LMAX - 16 + spread, LMAX - 16 - spread], axis=-1).reshape(N_SHARD, N_DP, SEQ_OWN)
    hot_first = jax.random.randint(key_start, (N_SHARD, 1, 1), 0, N_DP, dtype=jnp.int32)
    crowded = (owner_ids < SEQ_OWN)[None, :, None]
    source = jnp.where(crowded, (hot_first + piece_ids[None, None, :]) % N_DP, (owner_ids[None, :, None] + piece_ids[None, None, :]) % N_DP)
    piece_hits = source[:, None, :, :] == owner_ids[None, :, None, None]
    piece_len = jnp.sum(jnp.where(piece_hits, piece_sizes[:, None, :, :], 0), axis=-1).astype(jnp.int32)
    piece_ends = jnp.cumsum(piece_len, axis=-1).astype(jnp.int32)
    segment_starts = piece_ends - piece_len
    row_ids = jnp.arange(LSLOT, dtype=jnp.int32)
    target = jnp.sum((piece_ends[:, :, None, :] <= row_ids[None, None, :, None]).astype(jnp.int32), axis=-1)
    row_alive = target < N_DP
    owner_safe = jnp.minimum(target, N_DP - 1)
    row_start = jnp.take_along_axis(segment_starts, owner_safe, axis=-1)
    row_len = jnp.where(row_alive, jnp.take_along_axis(piece_len, owner_safe, axis=-1), 0)
    row_position = jnp.where(row_alive, row_ids[None, None, :] - row_start, 0)
    time_bits = jax.random.randint(key_time, (N_SHARD, N_DP, N_DP), 0, 1 << 20, dtype=jnp.int32)
    seq_time = 1 + time_bits % jnp.maximum(piece_len, 1)
    row_time = jnp.where(row_alive, jnp.take_along_axis(seq_time, owner_safe, axis=-1), 0)
    rank_keys = jax.random.randint(key_rank, (N_SHARD, N_DP, LSLOT), 0, 1 << 20, dtype=jnp.int32)
    composite = target * (1 << 20) + rank_keys
    sorted_ids = jnp.argsort(composite, axis=-1, stable=True)
    row_rank = jnp.argsort(sorted_ids, axis=-1, stable=True).astype(jnp.int32)
    row_order = jnp.where(row_alive, row_rank - row_start, 0)
    return (target, row_position, row_len, row_order, row_time)


def flatten_layout(values):
    return jnp.transpose(values, (1, 0, 2)).reshape(-1).astype(jnp.int32)


def draw_destination(key, part):
    return flatten_layout(build_layout(key)[0])


def draw_position(key, part):
    return flatten_layout(build_layout(key)[1])


def draw_length(key, part):
    return flatten_layout(build_layout(key)[2])


def draw_unmask_order(key, part):
    return flatten_layout(build_layout(key)[3])


def draw_timestep(key, part):
    return flatten_layout(build_layout(key)[4])


def strengthened(array, own_key, source, target, shards_of, factor):
    def block_of(dim):
        return (jnp.arange(array.shape[dim]) // (array.shape[dim] // shards_of)).reshape((-1,) + (1,) * (array.ndim - 1 - dim))

    first = jax.random.permutation(own_key, shards_of)[block_of(target)]
    other_side = (block_of(target) + shards_of // 2) % shards_of
    return jnp.where((block_of(source) == first) | (block_of(source) == other_side), factor * array, array)


def shard_levels(stream_key, shape, shards, low, largest):
    def one(axis_at, parts):
        draws = jax.random.uniform(jax.random.fold_in(jax.random.fold_in(stream_key, 6), axis_at), (parts,), jnp.float32, low / len(shards), largest / len(shards))
        return jnp.repeat(jnp.exp(draws), shape[axis_at] // parts).reshape((-1,) + (1,) * (len(shape) - axis_at - 1))

    loudness = one(*shards[0])
    for cut in shards[1:]:
        loudness = loudness * one(*cut)
    return loudness


def noise(own_key, dims, scale, limit, cuts=(), kind=jnp.bfloat16):
    drawn = jax.random.normal(own_key, dims, jnp.float32) * scale
    if len(cuts) > 0:
        drawn = shard_levels(own_key, dims, cuts, -0.22, 0.18) * drawn
    return jnp.clip(drawn, min=-limit, max=limit).astype(kind)


def noise_with(key, extent, scale, most, shards, heavy, kind=jnp.bfloat16):
    drawn = scale * jax.random.normal(key, extent, jnp.float32)
    if shards:
        drawn = drawn * shard_levels(key, extent, shards, -0.22, 0.18)
    return jnp.clip(strengthened(drawn, jax.random.fold_in(key, 3), *heavy), -most, most).astype(kind)


def setup_inputs(seed: int = 0) -> dict:
    keys = jax.random.split(jax.random.key(seed), 15)
    return {
        "embedded": noise(keys[0], (LOAD_ROWS, D), 1.0, 6.0, ((0, 32),)),
        "mask_token_embedding": noise(keys[1], (D,), 1.0, 5.0),
        "destination": draw_destination(jax.random.fold_in(keys[14], 71), 0),
        "position": draw_position(jax.random.fold_in(keys[14], 71), 0),
        "length": draw_length(jax.random.fold_in(keys[14], 71), 0),
        "unmask_order": draw_unmask_order(jax.random.fold_in(keys[14], 71), 0),
        "timestep": draw_timestep(jax.random.fold_in(keys[14], 71), 0),
        "upstream": noise_with(keys[7], (OWN_ROWS, D), 0.05, 0.29882812, ((0, 32),), (0, 1, 32, 2.75)),
        "gain_in": jnp.clip(1.0 + 0.12 * jax.random.normal(keys[8], (D,), jnp.float32), 0.4, 1.6),
        "weight_in": noise(keys[9], (D, H), D ** -0.5, 0.15625),
        "gain_mid": jnp.clip(1.0 + 0.12 * jax.random.normal(keys[10], (H,), jnp.float32), 0.4, 1.6),
        "weight_conv": noise(keys[11], (H, KERNEL_TAPS, H), (KERNEL_TAPS * H) ** -0.5, 0.109375),
        "gain_out": jnp.clip(1.0 + 0.12 * jax.random.normal(keys[12], (H,), jnp.float32), 0.4, 1.6),
        "weight_out": noise(keys[13], (D, H), H ** -0.5, 0.25),
    }


EPS = 1e-05

def normalized_activation(values, gain_vec):
    row_mean = lax.optimization_barrier(jnp.mean(values, axis=-1, keepdims=True))
    centred = values - row_mean
    row_var = lax.optimization_barrier(jnp.mean(centred * centred, axis=-1, keepdims=True))
    return jax.nn.gelu(centred * lax.rsqrt(row_var + EPS) * gain_vec, approximate=False)

def raw_shift(values, offset):
    if offset > 0:
        filler = jnp.zeros((offset, values.shape[1]), values.dtype)
        return jnp.concatenate([values[offset:], filler], axis=0)
    if offset < 0:
        filler = jnp.zeros((-offset, values.shape[1]), values.dtype)
        return jnp.concatenate([filler, values[:offset]], axis=0)
    return values

def contract_rows(left, right):
    return lax.dot_general(left, right, (((0,), (0,)), ((), ())), preferred_element_type=jnp.float32)

def contract_cols(left, right):
    return lax.dot_general(left, right, (((1,), (1,)), ((), ())), preferred_element_type=jnp.float32)

def layer_grads(owner_input, upstream, owner_position, owner_length, gain_in, weight_in, gain_mid, weight_conv, gain_out, weight_out):
    widened_input = owner_input.astype(jnp.float32)
    first_f32, pull_in = jax.vjp(lambda value: normalized_activation(value, gain_in), widened_input)
    first_act = first_f32.astype(jnp.bfloat16)
    hidden = jnp.dot(first_act, weight_in, preferred_element_type=jnp.float32)
    mid_f32, pull_mid = jax.vjp(lambda value: normalized_activation(value, gain_mid), hidden)
    mid_act = mid_f32.astype(jnp.bfloat16)
    tap_offsets = [(kernel_tap_index - KERNEL_TAPS // 2) * DILATION_STEP for kernel_tap_index in range(KERNEL_TAPS)]
    tap_valid = [(owner_position + offset >= 0) & (owner_position + offset < owner_length) for offset in tap_offsets]
    tap_list = [jnp.where(tap_valid[kernel_tap_index][:, None], raw_shift(mid_act, tap_offsets[kernel_tap_index]), jnp.zeros_like(mid_act)) for kernel_tap_index in range(KERNEL_TAPS)]
    conv = jnp.dot(tap_list[0], weight_conv[:, 0, :], preferred_element_type=jnp.float32)
    for kernel_tap_index in range(1, KERNEL_TAPS):
        conv = conv + jnp.dot(tap_list[kernel_tap_index], weight_conv[:, kernel_tap_index, :], preferred_element_type=jnp.float32)
    out_f32, pull_out = jax.vjp(lambda value: normalized_activation(value, gain_out), conv)
    out_act = out_f32.astype(jnp.bfloat16)
    grad_out = contract_rows(upstream, out_act)
    out_cot = jnp.dot(upstream, weight_out, preferred_element_type=jnp.float32)
    conv_cot = pull_out(out_cot)[0].astype(jnp.bfloat16)
    grad_conv = jnp.stack([contract_rows(tap_list[kernel_tap_index], conv_cot) for kernel_tap_index in range(KERNEL_TAPS)], axis=1)
    mid_cot = jnp.zeros(mid_act.shape, jnp.float32)
    for kernel_tap_index in range(KERNEL_TAPS):
        back_term = contract_cols(conv_cot, weight_conv[:, kernel_tap_index, :])
        back_term = jnp.where(tap_valid[kernel_tap_index][:, None], back_term, jnp.zeros_like(back_term))
        mid_cot = mid_cot + raw_shift(back_term, -tap_offsets[kernel_tap_index])
    hidden_cot = pull_mid(mid_cot)[0].astype(jnp.bfloat16)
    grad_in = contract_rows(first_act, hidden_cot)
    input_cot = contract_cols(hidden_cot, weight_in)
    grad_input = (upstream.astype(jnp.float32) + pull_in(input_cot)[0]).astype(jnp.bfloat16)
    return (grad_input, grad_in, grad_conv, grad_out)

def reference(embedded, mask_token_embedding, destination, position, length, unmask_order, timestep, upstream, gain_in, weight_in, gain_mid, weight_conv, gain_out, weight_out):
    channels = embedded.shape[1]
    masked_input = jnp.where((unmask_order < timestep)[:, None], mask_token_embedding[None, :], embedded)

    def regroup(values, slots):
        tail = values.shape[1:]
        grouped = values.reshape((N_DP, N_SHARD, slots) + tail)
        return jnp.moveaxis(grouped, 1, 0).reshape((N_SHARD, N_DP * slots) + tail)

    def one_group(pieces):
        group_rows, group_dest, group_pos, group_len, group_up = pieces
        ordering = jnp.argsort(group_dest, stable=True)[:N_DP * TOK].astype(jnp.int32)
        return layer_grads(group_rows[ordering], group_up, group_pos[ordering], group_len[ordering], gain_in, weight_in, gain_mid, weight_conv, gain_out, weight_out)
    grouped_inputs = (regroup(masked_input, LSLOT), regroup(destination, LSLOT), regroup(position, LSLOT), regroup(length, LSLOT), regroup(upstream, TOK))
    grad_rows, grad_in, grad_conv, grad_out = lax.map(one_group, grouped_inputs)
    grad_input = jnp.moveaxis(grad_rows.reshape(N_SHARD, N_DP, TOK, channels), 0, 1).reshape(N_DP * N_SHARD * TOK, channels)
    return (grad_input, lax.optimization_barrier(jnp.sum(grad_in, axis=0)), lax.optimization_barrier(jnp.sum(grad_conv, axis=0)), lax.optimization_barrier(jnp.sum(grad_out, axis=0)))
```

```python
import jax
import jax.numpy as jnp
from jax import lax
from jax.experimental import pallas as pl
from jax.experimental.pallas import tpu as pltpu
import functools
from jax.sharding import PartitionSpec as P

KERNEL_TAPS = 5
DILATION_STEP = 16
LMAX = 80


EPS = 1e-05


def normalized_activation(values, gain_vec):
    row_mean = jnp.mean(values, axis=-1, keepdims=True)
    centred = values - row_mean
    row_var = jnp.mean(centred * centred, axis=-1, keepdims=True)
    return jax.nn.gelu(centred * lax.rsqrt(row_var + EPS) * gain_vec, approximate=False)


def raw_shift(values, offset):
    if offset > 0:
        filler = jnp.zeros((offset, values.shape[1]), values.dtype)
        return jnp.concatenate([values[offset:], filler], axis=0)
    if offset < 0:
        filler = jnp.zeros((-offset, values.shape[1]), values.dtype)
        return jnp.concatenate([filler, values[:offset]], axis=0)
    return values


def contract_rows(left, right):
    return lax.dot_general(
        left, right, (((0,), (0,)), ((), ())), preferred_element_type=jnp.float32
    )


def contract_cols(left, right):
    return lax.dot_general(
        left, right, (((1,), (1,)), ((), ())), preferred_element_type=jnp.float32
    )


def layer_grads(
    owner_input,
    upstream,
    owner_position,
    owner_length,
    gain_in,
    weight_in,
    gain_mid,
    weight_conv,
    gain_out,
    weight_out,
):
    widened_input = owner_input.astype(jnp.float32)
    first_f32, pull_in = jax.vjp(lambda value: normalized_activation(value, gain_in), widened_input)
    first_act = first_f32.astype(jnp.bfloat16)
    hidden = jnp.dot(first_act, weight_in, preferred_element_type=jnp.float32)
    mid_f32, pull_mid = jax.vjp(lambda value: normalized_activation(value, gain_mid), hidden)
    mid_act = mid_f32.astype(jnp.bfloat16)
    tap_offsets = [
        (kernel_tap_index - KERNEL_TAPS // 2) * DILATION_STEP
        for kernel_tap_index in range(KERNEL_TAPS)
    ]
    tap_valid = [
        (owner_position + offset >= 0) & (owner_position + offset < owner_length)
        for offset in tap_offsets
    ]
    tap_list = [
        jnp.where(
            tap_valid[kernel_tap_index][:, None],
            raw_shift(mid_act, tap_offsets[kernel_tap_index]),
            jnp.zeros_like(mid_act),
        )
        for kernel_tap_index in range(KERNEL_TAPS)
    ]
    conv = jnp.dot(tap_list[0], weight_conv[:, 0, :], preferred_element_type=jnp.float32)
    for kernel_tap_index in range(1, KERNEL_TAPS):
        conv = conv + jnp.dot(
            tap_list[kernel_tap_index],
            weight_conv[:, kernel_tap_index, :],
            preferred_element_type=jnp.float32,
        )
    out_f32, pull_out = jax.vjp(lambda value: normalized_activation(value, gain_out), conv)
    out_act = out_f32.astype(jnp.bfloat16)
    out_cot = jnp.dot(upstream, weight_out, preferred_element_type=jnp.float32)
    conv_cot = pull_out(out_cot)[0].astype(jnp.bfloat16)
    mid_cot = jnp.zeros(mid_act.shape, jnp.float32)
    for kernel_tap_index in range(KERNEL_TAPS):
        back_term = contract_cols(conv_cot, weight_conv[:, kernel_tap_index, :])
        back_term = jnp.where(
            tap_valid[kernel_tap_index][:, None], back_term, jnp.zeros_like(back_term)
        )
        mid_cot = mid_cot + raw_shift(back_term, -tap_offsets[kernel_tap_index])
    hidden_cot = pull_mid(mid_cot)[0].astype(jnp.bfloat16)
    input_cot = contract_cols(hidden_cot, weight_in)
    grad_input = (upstream.astype(jnp.float32) + pull_in(input_cot)[0]).astype(jnp.bfloat16)
    return (grad_input, first_act, mid_act, out_act, conv_cot, hidden_cot)


MESH = pl.DeviceIdType.MESH


def bit_orders(owners, groups):
    dp_bits = [("dp", i) for i in range(owners.bit_length() - 1)]
    sh_bits = [("shard", i) for i in range(groups.bit_length() - 1)]
    first, others = sh_bits[:1], sh_bits[1:]
    return (
        first + others + dp_bits,
        first + dp_bits[:1] + others + dp_bits[1:],
        first + dp_bits[1:] + others + dp_bits[:1],
    )


def place(order, owner, group):
    index = 0
    for axis, bit in order:
        index = index * 2 + (((owner if axis == "dp" else group) >> bit) & 1)
    return index


def chunk_rows(rows):
    unit = rows // 5
    return (2 * unit, 2 * unit, unit)


def round_up(value, multiple):
    return -(-value // multiple) * multiple


def placed(values, offset):
    low = offset // 128 * 128
    high = round_up(offset + values.shape[1], 128)
    parts = []
    if offset > low:
        parts.append(jnp.zeros((values.shape[0], offset - low), values.dtype))
    parts.append(values)
    if high > offset + values.shape[1]:
        parts.append(jnp.zeros((values.shape[0], high - offset - values.shape[1]), values.dtype))
    return low, (jnp.concatenate(parts, axis=1) if len(parts) > 1 else values)


def weight_terms_kernel(
    owners, groups, position, length, mid, conv_cot, first, hidden_cot, upstream, out_act, *outs
):
    taps = []
    for k in range(KERNEL_TAPS):
        offset = (k - KERNEL_TAPS // 2) * DILATION_STEP
        moved = position[...] + offset
        valid = (moved >= 0) & (moved < length[...])
        shifted = raw_shift(mid[...], offset).astype(jnp.float32)
        taps.append(jnp.where(valid, shifted, 0.0))
    narrow, wide = mid.shape[1] // owners, first.shape[1] // owners
    rows = conv_cot.shape[1] // groups
    width = outs[0].shape[2]
    conv_t, hidden_t, out_t = conv_cot[...].T, hidden_cot[...].T, out_act[...].T
    orders = bit_orders(owners, groups)
    for owner in range(owners):
        here = slice(owner * narrow, (owner + 1) * narrow)
        there = slice(owner * wide, (owner + 1) * wide)
        left = (
            (conv_t, jnp.concatenate([t[:, here] for t in taps], axis=1), 0),
            (hidden_t, first[:, there].astype(jnp.float32), KERNEL_TAPS * narrow),
            (out_t, upstream[:, there].astype(jnp.float32), KERNEL_TAPS * narrow + wide),
        )
        tiles = [None] * (width // 128)
        for right, values, offset in left:
            low, padded = placed(values, offset)
            term = jnp.dot(
                right, padded.astype(jnp.bfloat16), preferred_element_type=jnp.float32
            )
            for j in range(padded.shape[1] // 128):
                piece = term[:, j * 128 : (j + 1) * 128]
                at = low // 128 + j
                tiles[at] = piece if tiles[at] is None else tiles[at] + piece
        for j, tile in enumerate(tiles):
            tile = tile.astype(jnp.bfloat16)
            for group in range(groups):
                start = group * rows
                for order, out, count in zip(orders, outs, chunk_rows(rows)):
                    out[place(order, owner, group), :, j * 128 : (j + 1) * 128] = tile[
                        start : start + count
                    ]
                    start += count


def reduce_kernel(owners, groups, *refs):
    chunks = 3
    terms, outs = refs[:chunks], refs[chunks : 2 * chunks]
    got, sums = refs[2 * chunks : 3 * chunks], refs[3 * chunks : 4 * chunks]
    send_sem, recv_sem = refs[4 * chunks :]
    orders = bit_orders(owners, groups)
    steps = len(orders[0])
    me = {"dp": lax.axis_index("dp"), "shard": lax.axis_index("shard")}

    def bit_of(axis, bit):
        return lax.rem(me[axis] // (1 << bit), 2)

    def partner(axis, bit):
        other = me[axis] + (1 - 2 * bit_of(axis, bit)) * (1 << bit)
        return (other, me["shard"]) if axis == "dp" else (me["dp"], other)

    barrier = pltpu.get_barrier_semaphore()
    for axis, bit in orders[0]:
        pl.semaphore_signal(barrier, inc=1, device_id=partner(axis, bit), device_id_type=MESH)
    pl.semaphore_wait(barrier, steps)

    total = 1 << steps
    base, at = [], 0
    for t in range(steps):
        base.append(at)
        at += total >> (t + 1)

    def copy_of(c, t):
        half = total >> (t + 1)
        away = 1 - bit_of(*orders[c][t])
        source = terms[c] if t == 0 else sums[c]
        start = away * half if t == 0 else base[t - 1] + away * half
        return pltpu.make_async_remote_copy(
            src_ref=source.at[pl.ds(start, half)],
            dst_ref=got[c].at[pl.ds(base[t], half)],
            send_sem=send_sem.at[c, t],
            recv_sem=recv_sem.at[c, t],
            device_id=partner(*orders[c][t]),
            device_id_type=MESH,
        )

    def add(c, t, first, count):
        half = total >> (t + 1)
        kept = bit_of(*orders[c][t]) * half
        source = terms[c] if t == 0 else sums[c]
        offset = kept if t == 0 else base[t - 1] + kept

        def body(i, carry):
            at = first + i
            value = source[offset + at].astype(jnp.float32) + got[c][base[t] + at].astype(
                jnp.float32
            )
            if t == steps - 1:
                outs[c][...] = value
            else:
                sums[c][base[t] + at] = value.astype(jnp.bfloat16)
            return carry

        lax.fori_loop(0, count, body, 0)

    copies = [[copy_of(c, t) for t in range(steps)] for c in range(chunks)]
    for c in range(chunks):
        copies[c][0].start()
    for t in range(steps):
        for c in range(chunks):
            copies[c][t].wait_recv()
            half = total >> (t + 1)
            if t == steps - 1:
                add(c, t, 0, 1)
            else:
                nxt = bit_of(*orders[c][t + 1])
                add(c, t, (1 - nxt) * (half // 2), half // 2)
                copies[c][t + 1].start()
                add(c, t, nxt * (half // 2), half // 2)
    for c in range(chunks):
        for t in range(steps):
            copies[c][t].wait_send()


def local(
    embedded,
    mask_token_embedding,
    destination,
    position,
    length,
    unmask_order,
    timestep,
    upstream,
    gain_in,
    weight_in,
    gain_mid,
    weight_conv,
    gain_out,
    weight_out,
):
    channels = embedded.shape[1]
    owners, groups = lax.axis_size("dp"), lax.axis_size("shard")
    own_rows = upstream.shape[0]
    inner = weight_in.shape[1]
    masked_input = jnp.where(
        (unmask_order < timestep)[:, None], mask_token_embedding[None, :], embedded
    )
    depth = LMAX + 8
    slot = jnp.where(destination < owners, destination * depth + position, -1)
    pick = (jnp.arange(owners * depth, dtype=jnp.int32)[:, None] == slot[None, :]).astype(
        jnp.bfloat16
    )
    send_len = jnp.max(
        jnp.where(
            destination[None, :] == jnp.arange(owners, dtype=jnp.int32)[:, None],
            length[None, :],
            0,
        ),
        axis=1,
    )
    send = jnp.dot(pick, masked_input, preferred_element_type=jnp.float32)
    send = send.reshape(owners, depth, channels)
    in_block = jnp.arange(depth, dtype=jnp.int32)[None, :, None]
    send = jnp.where(
        in_block >= LMAX, send_len[:, None, None].astype(jnp.float32), send
    ).astype(jnp.bfloat16)
    got = lax.all_to_all(send, "dp", split_axis=0, concat_axis=0, tiled=True)
    got_len = got[:, LMAX, 0].astype(jnp.int32)
    ends = jnp.cumsum(got_len)
    starts = ends - got_len
    row = jnp.arange(own_rows, dtype=jnp.int32)
    mine = (row[:, None] >= starts[None, :]) & (row[:, None] < ends[None, :])
    bucket_pos = jnp.sum(jnp.where(mine, row[:, None] - starts[None, :], 0), axis=1)
    bucket_len = jnp.sum(jnp.where(mine, got_len[None, :], 0), axis=1)
    source = jnp.sum(
        jnp.where(mine, jnp.arange(owners, dtype=jnp.int32)[None, :] * depth, 0), axis=1
    )
    take = (
        (source + bucket_pos)[:, None] == jnp.arange(owners * depth, dtype=jnp.int32)[None, :]
    ).astype(jnp.bfloat16)
    bucket = jnp.dot(
        take, got.reshape(-1, channels), preferred_element_type=jnp.float32
    ).astype(jnp.bfloat16)
    grad_input, first_act, mid_act, out_act, conv_cot, hidden_cot = layer_grads(
        bucket,
        upstream,
        bucket_pos,
        bucket_len,
        gain_in,
        weight_in,
        gain_mid,
        weight_conv,
        gain_out,
        weight_out,
    )
    narrow, wide, rows = inner // owners, channels // owners, inner // groups
    width = round_up(KERNEL_TAPS * narrow + 2 * wide, 128)
    total = owners * groups
    vmem = pl.BlockSpec(memory_space=pltpu.VMEM)
    counts = chunk_rows(rows)
    terms = pl.pallas_call(
        functools.partial(weight_terms_kernel, owners, groups),
        out_shape=[jax.ShapeDtypeStruct((total, n, width), jnp.bfloat16) for n in counts],
        in_specs=[vmem] * 8,
        out_specs=[vmem] * 3,
        compiler_params=pltpu.CompilerParams(vmem_limit_bytes=60 * 1024 * 1024),
        name="weight_terms",
    )(
        bucket_pos[:, None],
        bucket_len[:, None],
        mid_act,
        conv_cot,
        first_act,
        hidden_cot,
        upstream,
        out_act,
    )
    steps = total.bit_length() - 1
    reduced = pl.pallas_call(
        functools.partial(reduce_kernel, owners, groups),
        out_shape=[jax.ShapeDtypeStruct((n, width), jnp.float32) for n in counts],
        in_specs=[vmem] * 3,
        out_specs=[vmem] * 3,
        scratch_shapes=[pltpu.VMEM((total - 1, n, width), jnp.bfloat16) for n in counts]
        + [pltpu.VMEM((total - 1, n, width), jnp.bfloat16) for n in counts]
        + [pltpu.SemaphoreType.DMA((3, steps)), pltpu.SemaphoreType.DMA((3, steps))],
        compiler_params=pltpu.CompilerParams(
            collective_id=0, has_side_effects=True, vmem_limit_bytes=60 * 1024 * 1024
        ),
        name="reduce_terms",
    )(*terms)
    reduced = jnp.concatenate(reduced, axis=0).T
    cut = KERNEL_TAPS * narrow
    reduced_conv = reduced[:cut].reshape(KERNEL_TAPS, narrow, rows).transpose(1, 0, 2)
    return (grad_input, reduced[cut : cut + wide], reduced_conv, reduced[cut + wide : cut + 2 * wide])


def solution(mesh):
    return jax.shard_map(
        local,
        mesh=mesh,
        in_specs=(
            P(("dp", "shard"), None),
            P(),
            P(("dp", "shard")),
            P(("dp", "shard")),
            P(("dp", "shard")),
            P(("dp", "shard")),
            P(("dp", "shard")),
            P(("dp", "shard"), None),
            P(),
            P(),
            P(),
            P(),
            P(),
            P(),
        ),
        out_specs=(
            P(("dp", "shard"), None),
            P("dp", "shard"),
            P("dp", None, "shard"),
            P("dp", "shard"),
        ),
        check_vma=False,
    )
```

```python
import jax
import jax.numpy as jnp
from jax import lax
from jax.experimental import pallas as pl
from jax.experimental.pallas import tpu as pltpu
import functools
from jax.sharding import PartitionSpec as P

KERNEL_TAPS = 5
DILATION_STEP = 16
LMAX = 80


EPS = 1e-05


def normalized_activation(values, gain_vec):
    row_mean = jnp.mean(values, axis=-1, keepdims=True)
    centred = values - row_mean
    row_var = jnp.mean(centred * centred, axis=-1, keepdims=True)
    return jax.nn.gelu(centred * lax.rsqrt(row_var + EPS) * gain_vec, approximate=False)


def raw_shift(values, offset):
    if offset > 0:
        filler = jnp.zeros((offset, values.shape[1]), values.dtype)
        return jnp.concatenate([values[offset:], filler], axis=0)
    if offset < 0:
        filler = jnp.zeros((-offset, values.shape[1]), values.dtype)
        return jnp.concatenate([filler, values[:offset]], axis=0)
    return values


def contract_rows(left, right):
    return lax.dot_general(
        left, right, (((0,), (0,)), ((), ())), preferred_element_type=jnp.float32
    )


def contract_cols(left, right):
    return lax.dot_general(
        left, right, (((1,), (1,)), ((), ())), preferred_element_type=jnp.float32
    )


def layer_grads(
    owner_input,
    upstream,
    owner_position,
    owner_length,
    gain_in,
    weight_in,
    gain_mid,
    weight_conv,
    gain_out,
    weight_out,
):
    widened_input = owner_input.astype(jnp.float32)
    first_f32 = normalized_activation(widened_input, gain_in)
    first_act = first_f32.astype(jnp.bfloat16)
    hidden = jnp.dot(first_act, weight_in, preferred_element_type=jnp.float32)
    mid_f32, pull_mid = jax.vjp(lambda value: normalized_activation(value, gain_mid), hidden)
    mid_act = mid_f32.astype(jnp.bfloat16)
    tap_offsets = [
        (kernel_tap_index - KERNEL_TAPS // 2) * DILATION_STEP
        for kernel_tap_index in range(KERNEL_TAPS)
    ]
    tap_valid = [
        (owner_position + offset >= 0) & (owner_position + offset < owner_length)
        for offset in tap_offsets
    ]
    tap_list = [
        jnp.where(
            tap_valid[kernel_tap_index][:, None],
            raw_shift(mid_act, tap_offsets[kernel_tap_index]),
            jnp.zeros_like(mid_act),
        )
        for kernel_tap_index in range(KERNEL_TAPS)
    ]
    conv = jnp.dot(tap_list[0], weight_conv[:, 0, :], preferred_element_type=jnp.float32)
    for kernel_tap_index in range(1, KERNEL_TAPS):
        conv = conv + jnp.dot(
            tap_list[kernel_tap_index],
            weight_conv[:, kernel_tap_index, :],
            preferred_element_type=jnp.float32,
        )
    out_f32, pull_out = jax.vjp(lambda value: normalized_activation(value, gain_out), conv)
    out_act = out_f32.astype(jnp.bfloat16)
    out_cot = jnp.dot(upstream, weight_out, preferred_element_type=jnp.float32)
    conv_cot = pull_out(out_cot)[0].astype(jnp.bfloat16)
    mid_cot = jnp.zeros(mid_act.shape, jnp.float32)
    for kernel_tap_index in range(KERNEL_TAPS):
        back_term = contract_cols(conv_cot, weight_conv[:, kernel_tap_index, :])
        back_term = jnp.where(
            tap_valid[kernel_tap_index][:, None], back_term, jnp.zeros_like(back_term)
        )
        mid_cot = mid_cot + raw_shift(back_term, -tap_offsets[kernel_tap_index])
    hidden_cot = pull_mid(mid_cot)[0].astype(jnp.bfloat16)
    return (first_act, mid_act, out_act, conv_cot, hidden_cot)


MESH = pl.DeviceIdType.MESH


def bit_orders(owners, groups):
    dp_bits = [("dp", i) for i in range(owners.bit_length() - 1)]
    sh_bits = [("shard", i) for i in range(groups.bit_length() - 1)]
    first, others = sh_bits[:1], sh_bits[1:]
    return (
        first + others + dp_bits,
        first + dp_bits[:1] + others + dp_bits[1:],
        first + dp_bits[1:] + others + dp_bits[:1],
    )


def chunk_rows(rows):
    unit = rows // 5
    return (2 * unit, 2 * unit, unit)


def round_up(value, multiple):
    return -(-value // multiple) * multiple


def placed(values, offset):
    low = offset // 128 * 128
    high = round_up(offset + values.shape[1], 128)
    parts = []
    if offset > low:
        parts.append(jnp.zeros((values.shape[0], offset - low), values.dtype))
    parts.append(values)
    if high > offset + values.shape[1]:
        parts.append(jnp.zeros((values.shape[0], high - offset - values.shape[1]), values.dtype))
    return low, (jnp.concatenate(parts, axis=1) if len(parts) > 1 else values)


FILL = 64.0
INV_SQRT2 = 0.7071067811865476
INV_SQRT_2PI = 0.3989422804014327
VMEM_LIMIT = 60 * 1024 * 1024


def flipped(index, mask):
    other, bit = index, 0
    while (mask >> bit) > 0:
        if (mask >> bit) & 1:
            other = other + (1 - 2 * lax.rem(index // (1 << bit), 2)) * (1 << bit)
        bit += 1
    return other


def dispatch_kernel(
    owners,
    destination,
    position,
    order,
    timestep,
    token,
    embedded,
    bucket,
    bucket_pos,
    bucket_len,
    sent,
    got,
    send_sem,
    recv_sem,
):
    me, group = lax.axis_index("dp"), lax.axis_index("shard")
    barrier = pltpu.get_barrier_semaphore()
    for j in range(1, owners):
        pl.semaphore_signal(
            barrier, inc=1, device_id=(flipped(me, j), group), device_id_type=MESH
        )
    slot = jnp.where(destination[...] < owners, destination[...] * LMAX + position[...], -1)
    hidden_slot = (order[...] < timestep[...]).astype(jnp.float32)

    def block_for(owner):
        rows = lax.broadcasted_iota(jnp.int32, (LMAX, slot.shape[1]), 0) + owner * LMAX
        pick = (rows == slot).astype(jnp.float32)
        live = jnp.sum(pick, axis=1, keepdims=True)
        masked = jnp.sum(pick * hidden_slot, axis=1, keepdims=True)
        block = jnp.dot(
            pick.astype(jnp.bfloat16), embedded[...], preferred_element_type=jnp.float32
        )
        block = jnp.where(masked > 0.5, token[...].astype(jnp.float32), block)
        return jnp.where(live > 0.5, block, FILL).astype(jnp.bfloat16)

    copies = []
    for j in range(owners - 1, 0, -1):
        other = flipped(me, j)
        sent[j] = block_for(other)
        if j == owners - 1:
            pl.semaphore_wait(barrier, owners - 1)
        copy = pltpu.make_async_remote_copy(
            src_ref=sent.at[j],
            dst_ref=got.at[me],
            send_sem=send_sem.at[j],
            recv_sem=recv_sem.at[j],
            device_id=(other, group),
            device_id_type=MESH,
        )
        copy.start()
        copies.append(copy)
    got[me] = block_for(me)
    for copy in copies:
        copy.wait_recv()
    lanes = lax.broadcasted_iota(jnp.int32, (1, owners * LMAX), 1)
    place_of = jnp.full((1, owners * LMAX), -1, jnp.int32)
    pos_of = jnp.zeros((1, owners * LMAX), jnp.float32)
    len_of = jnp.zeros((1, owners * LMAX), jnp.float32)
    start = jnp.zeros((1, 1), jnp.int32)
    for source in range(owners):
        marks = got[source, :, 0:128].astype(jnp.float32)[:, 0:1]
        count = jnp.sum((marks < FILL / 2).astype(jnp.float32), axis=0, keepdims=True)
        whole = count.astype(jnp.int32)
        inside = lanes - source * LMAX
        used = (inside >= 0) & (inside < whole)
        place_of = jnp.where(used, start + inside, place_of)
        pos_of = jnp.where(used, inside.astype(jnp.float32), pos_of)
        len_of = jnp.where(used, count, len_of)
        start = start + whole
    own = bucket.shape[0]
    take = (
        lax.broadcasted_iota(jnp.int32, (own, owners * LMAX), 0) == place_of
    ).astype(jnp.float32)
    bucket_pos[...] = jnp.sum(take * pos_of, axis=1, keepdims=True).astype(jnp.int32)
    bucket_len[...] = jnp.sum(take * len_of, axis=1, keepdims=True).astype(jnp.int32)
    bucket[...] = jnp.dot(
        take.astype(jnp.bfloat16),
        got[...].reshape(owners * LMAX, bucket.shape[1]),
        preferred_element_type=jnp.float32,
    ).astype(jnp.bfloat16)
    for copy in copies:
        copy.wait_send()


def gradient_kernel(
    owners,
    groups,
    position,
    length,
    mid,
    conv_cot,
    first,
    hidden_cot,
    upstream,
    out_act,
    weight_in,
    owner_input,
    gain_in,
    grad_input,
    grad_in,
    grad_conv,
    grad_out,
    *scratch,
):
    chunks = 3
    terms, got, sums = scratch[:chunks], scratch[chunks : 2 * chunks], scratch[2 * chunks : 9]
    lefts, rights, input_cot, send_sem, recv_sem = (
        scratch[9:12],
        scratch[12:15],
        scratch[15],
        scratch[16],
        scratch[17],
    )
    orders = bit_orders(owners, groups)
    steps = len(orders[0])
    total = 1 << steps
    me = {"dp": lax.axis_index("dp"), "shard": lax.axis_index("shard")}

    def bit_of(axis, bit):
        return lax.rem(me[axis] // (1 << bit), 2)

    def partner(axis, bit):
        other = me[axis] + (1 - 2 * bit_of(axis, bit)) * (1 << bit)
        return (other, me["shard"]) if axis == "dp" else (me["dp"], other)

    barrier = pltpu.get_barrier_semaphore()
    for axis, bit in orders[0]:
        pl.semaphore_signal(barrier, inc=1, device_id=partner(axis, bit), device_id_type=MESH)

    narrow, wide = mid.shape[1] // owners, first.shape[1] // owners
    rows = conv_cot.shape[1] // groups
    width = terms[0].shape[2]
    offsets = (0, KERNEL_TAPS * narrow, KERNEL_TAPS * narrow + wide)
    taps = []
    for k in range(KERNEL_TAPS):
        offset = (k - KERNEL_TAPS // 2) * DILATION_STEP
        moved = position[...] + offset
        valid = (moved >= 0) & (moved < length[...])
        shifted = raw_shift(mid[...], offset).astype(jnp.float32)
        taps.append(jnp.where(valid, shifted, 0.0))
    for right, values in zip(rights, (conv_cot, hidden_cot, out_act)):
        right[...] = values[...].T
    for owner in range(owners):
        here = slice(owner * narrow, (owner + 1) * narrow)
        there = slice(owner * wide, (owner + 1) * wide)
        parts = (
            jnp.concatenate([t[:, here] for t in taps], axis=1),
            first[:, there].astype(jnp.float32),
            upstream[:, there].astype(jnp.float32),
        )
        for left, values, offset in zip(lefts, parts, offsets):
            left[owner] = placed(values, offset)[1].astype(jnp.bfloat16)

    def half_terms(low_bit):
        starts = [(2 * i + low_bit) * rows for i in range(groups // 2)]

        def body(owner, carry):
            tiles = [None] * (width // 128)
            for left, right, offset in zip(lefts, rights, offsets):
                low = offset // 128
                picked = [right[pl.ds(pl.multiple_of(s, 16), rows), :] for s in starts]
                picked = picked[0] if len(picked) == 1 else jnp.concatenate(picked, axis=0)
                term = jnp.dot(picked, left[owner], preferred_element_type=jnp.float32)
                for j in range(left.shape[2] // 128):
                    piece = term[:, j * 128 : (j + 1) * 128]
                    held = tiles[low + j]
                    tiles[low + j] = piece if held is None else held + piece
            for j, tile in enumerate(tiles):
                tile = tile.astype(jnp.bfloat16)
                for i in range(groups // 2):
                    at = i * rows
                    for order, out in zip(orders, terms):
                        index = low_bit
                        for axis, bit in order[1:]:
                            if axis == "dp":
                                index = index * 2 + lax.rem(owner // (1 << bit), 2)
                            else:
                                index = index * 2 + (((2 * i) >> bit) & 1)
                        count = out.shape[1]
                        out[index, :, j * 128 : (j + 1) * 128] = tile[at : at + count]
                        at += count
            return carry

        lax.fori_loop(0, owners, body, 0)

    base, at = [], 0
    for t in range(steps):
        base.append(at)
        at += total >> (t + 1)

    def copy_of(c, t):
        half = total >> (t + 1)
        away = 1 - bit_of(*orders[c][t])
        source = terms[c] if t == 0 else sums[c]
        start = away * half if t == 0 else base[t - 1] + away * half
        return pltpu.make_async_remote_copy(
            src_ref=source.at[pl.ds(start, half)],
            dst_ref=got[c].at[pl.ds(base[t], half)],
            send_sem=send_sem.at[c, t],
            recv_sem=recv_sem.at[c, t],
            device_id=partner(*orders[c][t]),
            device_id_type=MESH,
        )

    def summed(c, t, at):
        half = total >> (t + 1)
        kept = bit_of(*orders[c][t]) * half
        source = terms[c] if t == 0 else sums[c]
        offset = kept if t == 0 else base[t - 1] + kept
        return source[offset + at].astype(jnp.float32) + got[c][base[t] + at].astype(jnp.float32)

    def add(c, t, first_block, count):
        def body(i, carry):
            at = first_block + i
            sums[c][base[t] + at] = summed(c, t, at).astype(jnp.bfloat16)
            return carry

        lax.fori_loop(0, count, body, 0)

    def input_gradient():
        input_cot[...] = contract_cols(hidden_cot[...], weight_in[...])
        step_rows = 16

        def body(i, carry):
            at = pl.ds(pl.multiple_of(i * step_rows, step_rows), step_rows)
            value = owner_input[at, :].astype(jnp.float32)
            centred = value - jnp.mean(value, axis=-1, keepdims=True)
            scale = lax.rsqrt(jnp.mean(centred * centred, axis=-1, keepdims=True) + EPS)
            normal = centred * scale
            gain = gain_in[...]
            scaled = normal * gain
            slope = 0.5 * (1.0 + lax.erf(scaled * INV_SQRT2)) + scaled * (
                INV_SQRT_2PI * jnp.exp(-0.5 * scaled * scaled)
            )
            cot = input_cot[at, :] * slope * gain
            grad = scale * (
                cot
                - jnp.mean(cot, axis=-1, keepdims=True)
                - normal * jnp.mean(cot * normal, axis=-1, keepdims=True)
            )
            grad_input[at, :] = (upstream[at, :].astype(jnp.float32) + grad).astype(
                jnp.bfloat16
            )
            return carry

        lax.fori_loop(0, owner_input.shape[0] // step_rows, body, 0)

    mine = bit_of(*orders[0][0])
    half_terms(1 - mine)
    pl.semaphore_wait(barrier, steps)
    copies = [[copy_of(c, t) for t in range(steps)] for c in range(chunks)]
    for c in range(chunks):
        copies[c][0].start()
    half_terms(mine)
    for t in range(steps - 1):
        half = total >> (t + 2)
        for c in range(chunks):
            copies[c][t].wait_recv()
            nxt = bit_of(*orders[c][t + 1])
            add(c, t, (1 - nxt) * half, half)
            copies[c][t + 1].start()
            add(c, t, nxt * half, half)
        if t == 0:
            input_gradient()
    finished = []
    for c in range(chunks):
        copies[c][steps - 1].wait_recv()
        finished.append(summed(c, steps - 1, 0))
    result = jnp.concatenate(finished, axis=0).T
    for k in range(KERNEL_TAPS):
        grad_conv[:, k, :] = result[k * narrow : (k + 1) * narrow]
    grad_in[...] = result[offsets[1] : offsets[1] + wide]
    grad_out[...] = result[offsets[2] : offsets[2] + wide]
    for c in range(chunks):
        for t in range(steps):
            copies[c][t].wait_send()


def local(
    embedded,
    mask_token_embedding,
    destination,
    position,
    length,
    unmask_order,
    timestep,
    upstream,
    gain_in,
    weight_in,
    gain_mid,
    weight_conv,
    gain_out,
    weight_out,
):
    channels = embedded.shape[1]
    owners, groups = lax.axis_size("dp"), lax.axis_size("shard")
    own_rows = upstream.shape[0]
    inner = weight_in.shape[1]
    vmem = pl.BlockSpec(memory_space=pltpu.VMEM)
    bucket, bucket_pos, bucket_len = pl.pallas_call(
        functools.partial(dispatch_kernel, owners),
        out_shape=[
            jax.ShapeDtypeStruct((own_rows, channels), jnp.bfloat16),
            jax.ShapeDtypeStruct((own_rows, 1), jnp.int32),
            jax.ShapeDtypeStruct((own_rows, 1), jnp.int32),
        ],
        in_specs=[vmem] * 6,
        out_specs=[vmem] * 3,
        scratch_shapes=[
            pltpu.VMEM((owners, LMAX, channels), jnp.bfloat16),
            pltpu.VMEM((owners, LMAX, channels), jnp.bfloat16),
            pltpu.SemaphoreType.DMA((owners,)),
            pltpu.SemaphoreType.DMA((owners,)),
        ],
        compiler_params=pltpu.CompilerParams(
            collective_id=1, has_side_effects=True, vmem_limit_bytes=VMEM_LIMIT
        ),
        name="dispatch",
    )(
        destination[None, :],
        position[None, :],
        unmask_order[None, :],
        timestep[None, :],
        mask_token_embedding[None, :],
        embedded,
    )
    first_act, mid_act, out_act, conv_cot, hidden_cot = layer_grads(
        bucket,
        upstream,
        bucket_pos[:, 0],
        bucket_len[:, 0],
        gain_in,
        weight_in,
        gain_mid,
        weight_conv,
        gain_out,
        weight_out,
    )
    narrow, wide, rows = inner // owners, channels // owners, inner // groups
    offsets = (0, KERNEL_TAPS * narrow, KERNEL_TAPS * narrow + wide)
    sizes = (KERNEL_TAPS * narrow, wide, wide)
    spans = [round_up(o + n, 128) - o // 128 * 128 for o, n in zip(offsets, sizes)]
    width = round_up(offsets[2] + wide, 128)
    total = owners * groups
    steps = total.bit_length() - 1
    counts = chunk_rows(rows)
    outs = pl.pallas_call(
        functools.partial(gradient_kernel, owners, groups),
        out_shape=[
            jax.ShapeDtypeStruct((own_rows, channels), jnp.bfloat16),
            jax.ShapeDtypeStruct((wide, rows), jnp.float32),
            jax.ShapeDtypeStruct((narrow, KERNEL_TAPS, rows), jnp.float32),
            jax.ShapeDtypeStruct((wide, rows), jnp.float32),
        ],
        in_specs=[vmem] * 11,
        out_specs=[vmem] * 4,
        scratch_shapes=[pltpu.VMEM((total, n, width), jnp.bfloat16) for n in counts]
        + [pltpu.VMEM((total - 1, n, width), jnp.bfloat16) for n in counts]
        + [pltpu.VMEM((total - 1, n, width), jnp.bfloat16) for n in counts]
        + [pltpu.VMEM((owners, own_rows, n), jnp.bfloat16) for n in spans]
        + [pltpu.VMEM((inner, own_rows), jnp.bfloat16)] * 3
        + [pltpu.VMEM((own_rows, channels), jnp.float32)]
        + [pltpu.SemaphoreType.DMA((3, steps)), pltpu.SemaphoreType.DMA((3, steps))],
        compiler_params=pltpu.CompilerParams(
            collective_id=0, has_side_effects=True, vmem_limit_bytes=VMEM_LIMIT
        ),
        name="gradients",
    )(
        bucket_pos,
        bucket_len,
        mid_act,
        conv_cot,
        first_act,
        hidden_cot,
        upstream,
        out_act,
        weight_in,
        bucket,
        gain_in[None, :],
    )
    return tuple(outs)


def solution(mesh):
    return jax.shard_map(
        local,
        mesh=mesh,
        in_specs=(
            P(("dp", "shard"), None),
            P(),
            P(("dp", "shard")),
            P(("dp", "shard")),
            P(("dp", "shard")),
            P(("dp", "shard")),
            P(("dp", "shard")),
            P(("dp", "shard"), None),
            P(),
            P(),
            P(),
            P(),
            P(),
            P(),
        ),
        out_specs=(
            P(("dp", "shard"), None),
            P("dp", "shard"),
            P("dp", None, "shard"),
            P("dp", "shard"),
        ),
        check_vma=False,
    )
```

```python
import jax
import jax.numpy as jnp
from jax import lax
from jax.experimental import pallas as pl
from jax.experimental.pallas import tpu as pltpu
import functools
from jax.sharding import PartitionSpec as P

KERNEL_TAPS = 5
DILATION_STEP = 16
LMAX = 80


EPS = 1e-05


def normalized_activation(values, gain_vec):
    row_mean = jnp.mean(values, axis=-1, keepdims=True)
    centred = values - row_mean
    row_var = jnp.mean(centred * centred, axis=-1, keepdims=True)
    return jax.nn.gelu(centred * lax.rsqrt(row_var + EPS) * gain_vec, approximate=False)


def raw_shift(values, offset):
    if offset > 0:
        filler = jnp.zeros((offset, values.shape[1]), values.dtype)
        return jnp.concatenate([values[offset:], filler], axis=0)
    if offset < 0:
        filler = jnp.zeros((-offset, values.shape[1]), values.dtype)
        return jnp.concatenate([filler, values[:offset]], axis=0)
    return values


def contract_rows(left, right):
    return lax.dot_general(
        left, right, (((0,), (0,)), ((), ())), preferred_element_type=jnp.float32
    )


def contract_cols(left, right):
    return lax.dot_general(
        left, right, (((1,), (1,)), ((), ())), preferred_element_type=jnp.float32
    )


def layer_grads(
    first_act,
    mid_act,
    upstream,
    owner_position,
    owner_length,
    weight_in,
    gain_mid,
    weight_conv,
    gain_out,
    weight_out,
):
    hidden = jnp.dot(first_act, weight_in, preferred_element_type=jnp.float32)
    _, pull_mid = jax.vjp(lambda value: normalized_activation(value, gain_mid), hidden)
    tap_offsets = [
        (kernel_tap_index - KERNEL_TAPS // 2) * DILATION_STEP
        for kernel_tap_index in range(KERNEL_TAPS)
    ]
    tap_valid = [
        (owner_position + offset >= 0) & (owner_position + offset < owner_length)
        for offset in tap_offsets
    ]
    tap_list = [
        jnp.where(
            tap_valid[kernel_tap_index][:, None],
            raw_shift(mid_act, tap_offsets[kernel_tap_index]),
            jnp.zeros_like(mid_act),
        )
        for kernel_tap_index in range(KERNEL_TAPS)
    ]
    conv = jnp.dot(tap_list[0], weight_conv[:, 0, :], preferred_element_type=jnp.float32)
    for kernel_tap_index in range(1, KERNEL_TAPS):
        conv = conv + jnp.dot(
            tap_list[kernel_tap_index],
            weight_conv[:, kernel_tap_index, :],
            preferred_element_type=jnp.float32,
        )
    out_f32, pull_out = jax.vjp(lambda value: normalized_activation(value, gain_out), conv)
    out_act = out_f32.astype(jnp.bfloat16)
    out_cot = jnp.dot(upstream, weight_out, preferred_element_type=jnp.float32)
    conv_cot = pull_out(out_cot)[0].astype(jnp.bfloat16)
    mid_cot = jnp.zeros(mid_act.shape, jnp.float32)
    for kernel_tap_index in range(KERNEL_TAPS):
        back_term = contract_cols(conv_cot, weight_conv[:, kernel_tap_index, :])
        back_term = jnp.where(
            tap_valid[kernel_tap_index][:, None], back_term, jnp.zeros_like(back_term)
        )
        mid_cot = mid_cot + raw_shift(back_term, -tap_offsets[kernel_tap_index])
    hidden_cot = pull_mid(mid_cot)[0].astype(jnp.bfloat16)
    return (out_act, conv_cot, hidden_cot)


MESH = pl.DeviceIdType.MESH


def bit_orders(owners, groups):
    dp_bits = [("dp", i) for i in range(owners.bit_length() - 1)]
    sh_bits = [("shard", i) for i in range(groups.bit_length() - 1)]
    first, others = sh_bits[:1], sh_bits[1:]
    return (
        first + others + dp_bits,
        first + dp_bits[:1] + others + dp_bits[1:],
        first + dp_bits[1:] + others + dp_bits[:1],
    )


def chunk_rows(rows):
    unit = rows // 5
    return (2 * unit, 2 * unit, unit)


def round_up(value, multiple):
    return -(-value // multiple) * multiple


def placed(values, offset):
    low = offset // 128 * 128
    high = round_up(offset + values.shape[1], 128)
    parts = []
    if offset > low:
        parts.append(jnp.zeros((values.shape[0], offset - low), values.dtype))
    parts.append(values)
    if high > offset + values.shape[1]:
        parts.append(jnp.zeros((values.shape[0], high - offset - values.shape[1]), values.dtype))
    return low, (jnp.concatenate(parts, axis=1) if len(parts) > 1 else values)


FILL = 64.0
INV_SQRT2 = 0.7071067811865476
INV_SQRT_2PI = 0.3989422804014327
VMEM_LIMIT = 60 * 1024 * 1024


def flipped(index, mask):
    other, bit = index, 0
    while (mask >> bit) > 0:
        if (mask >> bit) & 1:
            other = other + (1 - 2 * lax.rem(index // (1 << bit), 2)) * (1 << bit)
        bit += 1
    return other


def activated(value, gain):
    centred = value - jnp.mean(value, axis=-1, keepdims=True)
    scale = lax.rsqrt(jnp.mean(centred * centred, axis=-1, keepdims=True) + EPS)
    scaled = centred * scale * gain
    return 0.5 * scaled * (1.0 + lax.erf(scaled * INV_SQRT2))


def dispatch_kernel(
    owners,
    destination,
    position,
    order,
    timestep,
    token,
    embedded,
    gain_in,
    weight_in,
    gain_mid,
    bucket,
    first,
    mid,
    bucket_pos,
    bucket_len,
    sent,
    got,
    got_first,
    got_mid,
    hidden,
    send_sem,
    recv_sem,
):
    me, group = lax.axis_index("dp"), lax.axis_index("shard")
    barrier = pltpu.get_barrier_semaphore()
    for j in range(1, owners):
        pl.semaphore_signal(
            barrier, inc=1, device_id=(flipped(me, j), group), device_id_type=MESH
        )
    slot = jnp.where(destination[...] < owners, destination[...] * LMAX + position[...], -1)
    hidden_slot = (order[...] < timestep[...]).astype(jnp.float32)

    def block_for(owner):
        rows = lax.broadcasted_iota(jnp.int32, (LMAX, slot.shape[1]), 0) + owner * LMAX
        pick = (rows == slot).astype(jnp.float32)
        live = jnp.sum(pick, axis=1, keepdims=True)
        masked = jnp.sum(pick * hidden_slot, axis=1, keepdims=True)
        block = jnp.dot(
            pick.astype(jnp.bfloat16), embedded[...], preferred_element_type=jnp.float32
        )
        block = jnp.where(masked > 0.5, token[...].astype(jnp.float32), block)
        return jnp.where(live > 0.5, block, FILL).astype(jnp.bfloat16)

    copies = []
    for j in range(owners - 1, 0, -1):
        other = flipped(me, j)
        sent[j] = block_for(other)
        if j == owners - 1:
            pl.semaphore_wait(barrier, owners - 1)
        copy = pltpu.make_async_remote_copy(
            src_ref=sent.at[j],
            dst_ref=got.at[me],
            send_sem=send_sem.at[j],
            recv_sem=recv_sem.at[j],
            device_id=(other, group),
            device_id_type=MESH,
        )
        copy.start()
        copies.append(copy)
    got[me] = block_for(me)

    def forward(source):
        step_rows = 16

        def enter(i, carry):
            at = pl.ds(pl.multiple_of(i * step_rows, step_rows), step_rows)
            value = got[source, at, :].astype(jnp.float32)
            got_first[source, at, :] = activated(value, gain_in[...]).astype(jnp.bfloat16)
            return carry

        def middle(i, carry):
            at = pl.ds(pl.multiple_of(i * step_rows, step_rows), step_rows)
            got_mid[source, at, :] = activated(hidden[at, :], gain_mid[...]).astype(
                jnp.bfloat16
            )
            return carry

        lax.fori_loop(0, LMAX // step_rows, enter, 0)
        hidden[...] = jnp.dot(
            got_first[source], weight_in[...], preferred_element_type=jnp.float32
        )
        lax.fori_loop(0, LMAX // step_rows, middle, 0)

    forward(me)
    for j, copy in zip(range(owners - 1, 0, -1), copies):
        copy.wait_recv()
        forward(flipped(me, j))
    lanes = lax.broadcasted_iota(jnp.int32, (1, owners * LMAX), 1)
    place_of = jnp.full((1, owners * LMAX), -1, jnp.int32)
    pos_of = jnp.zeros((1, owners * LMAX), jnp.float32)
    len_of = jnp.zeros((1, owners * LMAX), jnp.float32)
    start = jnp.zeros((1, 1), jnp.int32)
    for source in range(owners):
        marks = got[source, :, 0:128].astype(jnp.float32)[:, 0:1]
        count = jnp.sum((marks < FILL / 2).astype(jnp.float32), axis=0, keepdims=True)
        whole = count.astype(jnp.int32)
        inside = lanes - source * LMAX
        used = (inside >= 0) & (inside < whole)
        place_of = jnp.where(used, start + inside, place_of)
        pos_of = jnp.where(used, inside.astype(jnp.float32), pos_of)
        len_of = jnp.where(used, count, len_of)
        start = start + whole
    own = bucket.shape[0]
    take = (
        lax.broadcasted_iota(jnp.int32, (own, owners * LMAX), 0) == place_of
    ).astype(jnp.float32)
    bucket_pos[...] = jnp.sum(take * pos_of, axis=1, keepdims=True).astype(jnp.int32)
    bucket_len[...] = jnp.sum(take * len_of, axis=1, keepdims=True).astype(jnp.int32)
    take = take.astype(jnp.bfloat16)
    for result, blocks in ((bucket, got), (first, got_first), (mid, got_mid)):
        result[...] = jnp.dot(
            take,
            blocks[...].reshape(owners * LMAX, result.shape[1]),
            preferred_element_type=jnp.float32,
        ).astype(jnp.bfloat16)
    for copy in copies:
        copy.wait_send()


def gradient_kernel(
    owners,
    groups,
    position,
    length,
    mid,
    conv_cot,
    first,
    hidden_cot,
    upstream,
    out_act,
    weight_in,
    owner_input,
    gain_in,
    grad_input,
    grad_in,
    grad_conv,
    grad_out,
    *scratch,
):
    chunks = 3
    terms, got, sums = scratch[:chunks], scratch[chunks : 2 * chunks], scratch[2 * chunks : 9]
    lefts, rights, input_cot, send_sem, recv_sem = (
        scratch[9:12],
        scratch[12:15],
        scratch[15],
        scratch[16],
        scratch[17],
    )
    orders = bit_orders(owners, groups)
    steps = len(orders[0])
    total = 1 << steps
    me = {"dp": lax.axis_index("dp"), "shard": lax.axis_index("shard")}

    def bit_of(axis, bit):
        return lax.rem(me[axis] // (1 << bit), 2)

    def partner(axis, bit):
        other = me[axis] + (1 - 2 * bit_of(axis, bit)) * (1 << bit)
        return (other, me["shard"]) if axis == "dp" else (me["dp"], other)

    barrier = pltpu.get_barrier_semaphore()
    for axis, bit in orders[0]:
        pl.semaphore_signal(barrier, inc=1, device_id=partner(axis, bit), device_id_type=MESH)

    narrow, wide = mid.shape[1] // owners, first.shape[1] // owners
    rows = conv_cot.shape[1] // groups
    width = terms[0].shape[2]
    offsets = (0, KERNEL_TAPS * narrow, KERNEL_TAPS * narrow + wide)
    taps = []
    for k in range(KERNEL_TAPS):
        offset = (k - KERNEL_TAPS // 2) * DILATION_STEP
        moved = position[...] + offset
        valid = (moved >= 0) & (moved < length[...])
        shifted = raw_shift(mid[...], offset).astype(jnp.float32)
        taps.append(jnp.where(valid, shifted, 0.0))
    for right, values in zip(rights, (conv_cot, hidden_cot, out_act)):
        right[...] = values[...].T
    for owner in range(owners):
        here = slice(owner * narrow, (owner + 1) * narrow)
        there = slice(owner * wide, (owner + 1) * wide)
        parts = (
            jnp.concatenate([t[:, here] for t in taps], axis=1),
            first[:, there].astype(jnp.float32),
            upstream[:, there].astype(jnp.float32),
        )
        for left, values, offset in zip(lefts, parts, offsets):
            left[owner] = placed(values, offset)[1].astype(jnp.bfloat16)

    def half_terms(low_bit):
        starts = [(2 * i + low_bit) * rows for i in range(groups // 2)]

        def body(owner, carry):
            tiles = [None] * (width // 128)
            for left, right, offset in zip(lefts, rights, offsets):
                low = offset // 128
                picked = [right[pl.ds(pl.multiple_of(s, 16), rows), :] for s in starts]
                picked = picked[0] if len(picked) == 1 else jnp.concatenate(picked, axis=0)
                term = jnp.dot(picked, left[owner], preferred_element_type=jnp.float32)
                for j in range(left.shape[2] // 128):
                    piece = term[:, j * 128 : (j + 1) * 128]
                    held = tiles[low + j]
                    tiles[low + j] = piece if held is None else held + piece
            for j, tile in enumerate(tiles):
                tile = tile.astype(jnp.bfloat16)
                for i in range(groups // 2):
                    at = i * rows
                    for order, out in zip(orders, terms):
                        index = low_bit
                        for axis, bit in order[1:]:
                            if axis == "dp":
                                index = index * 2 + lax.rem(owner // (1 << bit), 2)
                            else:
                                index = index * 2 + (((2 * i) >> bit) & 1)
                        count = out.shape[1]
                        out[index, :, j * 128 : (j + 1) * 128] = tile[at : at + count]
                        at += count
            return carry

        lax.fori_loop(0, owners, body, 0)

    base, at = [], 0
    for t in range(steps):
        base.append(at)
        at += total >> (t + 1)

    def copy_of(c, t):
        half = total >> (t + 1)
        away = 1 - bit_of(*orders[c][t])
        source = terms[c] if t == 0 else sums[c]
        start = away * half if t == 0 else base[t - 1] + away * half
        return pltpu.make_async_remote_copy(
            src_ref=source.at[pl.ds(start, half)],
            dst_ref=got[c].at[pl.ds(base[t], half)],
            send_sem=send_sem.at[c, t],
            recv_sem=recv_sem.at[c, t],
            device_id=partner(*orders[c][t]),
            device_id_type=MESH,
        )

    def summed(c, t, at):
        half = total >> (t + 1)
        kept = bit_of(*orders[c][t]) * half
        source = terms[c] if t == 0 else sums[c]
        offset = kept if t == 0 else base[t - 1] + kept
        return source[offset + at].astype(jnp.float32) + got[c][base[t] + at].astype(jnp.float32)

    def add(c, t, first_block, count):
        def body(i, carry):
            at = first_block + i
            sums[c][base[t] + at] = summed(c, t, at).astype(jnp.bfloat16)
            return carry

        lax.fori_loop(0, count, body, 0)

    def input_gradient():
        input_cot[...] = contract_cols(hidden_cot[...], weight_in[...])
        step_rows = 16

        def body(i, carry):
            at = pl.ds(pl.multiple_of(i * step_rows, step_rows), step_rows)
            value = owner_input[at, :].astype(jnp.float32)
            centred = value - jnp.mean(value, axis=-1, keepdims=True)
            scale = lax.rsqrt(jnp.mean(centred * centred, axis=-1, keepdims=True) + EPS)
            normal = centred * scale
            gain = gain_in[...]
            scaled = normal * gain
            slope = 0.5 * (1.0 + lax.erf(scaled * INV_SQRT2)) + scaled * (
                INV_SQRT_2PI * jnp.exp(-0.5 * scaled * scaled)
            )
            cot = input_cot[at, :] * slope * gain
            grad = scale * (
                cot
                - jnp.mean(cot, axis=-1, keepdims=True)
                - normal * jnp.mean(cot * normal, axis=-1, keepdims=True)
            )
            grad_input[at, :] = (upstream[at, :].astype(jnp.float32) + grad).astype(
                jnp.bfloat16
            )
            return carry

        lax.fori_loop(0, owner_input.shape[0] // step_rows, body, 0)

    mine = bit_of(*orders[0][0])
    half_terms(1 - mine)
    pl.semaphore_wait(barrier, steps)
    copies = [[copy_of(c, t) for t in range(steps)] for c in range(chunks)]
    for c in range(chunks):
        copies[c][0].start()
    half_terms(mine)
    for t in range(steps - 1):
        half = total >> (t + 2)
        for c in range(chunks):
            copies[c][t].wait_recv()
            nxt = bit_of(*orders[c][t + 1])
            add(c, t, (1 - nxt) * half, half)
            copies[c][t + 1].start()
            add(c, t, nxt * half, half)
        if t == 0:
            input_gradient()
    finished = []
    for c in range(chunks):
        copies[c][steps - 1].wait_recv()
        finished.append(summed(c, steps - 1, 0))
    result = jnp.concatenate(finished, axis=0).T
    for k in range(KERNEL_TAPS):
        grad_conv[k] = result[k * narrow : (k + 1) * narrow]
    grad_in[...] = result[offsets[1] : offsets[1] + wide]
    grad_out[...] = result[offsets[2] : offsets[2] + wide]
    for c in range(chunks):
        for t in range(steps):
            copies[c][t].wait_send()


def local(
    embedded,
    mask_token_embedding,
    destination,
    position,
    length,
    unmask_order,
    timestep,
    upstream,
    gain_in,
    weight_in,
    gain_mid,
    weight_conv,
    gain_out,
    weight_out,
):
    channels = embedded.shape[1]
    owners, groups = lax.axis_size("dp"), lax.axis_size("shard")
    own_rows = upstream.shape[0]
    inner = weight_in.shape[1]
    vmem = pl.BlockSpec(memory_space=pltpu.VMEM)
    bucket, first_act, mid_act, bucket_pos, bucket_len = pl.pallas_call(
        functools.partial(dispatch_kernel, owners),
        out_shape=[
            jax.ShapeDtypeStruct((own_rows, channels), jnp.bfloat16),
            jax.ShapeDtypeStruct((own_rows, channels), jnp.bfloat16),
            jax.ShapeDtypeStruct((own_rows, inner), jnp.bfloat16),
            jax.ShapeDtypeStruct((own_rows, 1), jnp.int32),
            jax.ShapeDtypeStruct((own_rows, 1), jnp.int32),
        ],
        in_specs=[vmem] * 9,
        out_specs=[vmem] * 5,
        scratch_shapes=[
            pltpu.VMEM((owners, LMAX, channels), jnp.bfloat16),
            pltpu.VMEM((owners, LMAX, channels), jnp.bfloat16),
            pltpu.VMEM((owners, LMAX, channels), jnp.bfloat16),
            pltpu.VMEM((owners, LMAX, inner), jnp.bfloat16),
            pltpu.VMEM((LMAX, inner), jnp.float32),
            pltpu.SemaphoreType.DMA((owners,)),
            pltpu.SemaphoreType.DMA((owners,)),
        ],
        compiler_params=pltpu.CompilerParams(
            collective_id=1, has_side_effects=True, vmem_limit_bytes=VMEM_LIMIT
        ),
        name="dispatch",
    )(
        destination[None, :],
        position[None, :],
        unmask_order[None, :],
        timestep[None, :],
        mask_token_embedding[None, :],
        embedded,
        gain_in[None, :],
        weight_in,
        gain_mid[None, :],
    )
    out_act, conv_cot, hidden_cot = layer_grads(
        first_act,
        mid_act,
        upstream,
        bucket_pos[:, 0],
        bucket_len[:, 0],
        weight_in,
        gain_mid,
        weight_conv,
        gain_out,
        weight_out,
    )
    narrow, wide, rows = inner // owners, channels // owners, inner // groups
    offsets = (0, KERNEL_TAPS * narrow, KERNEL_TAPS * narrow + wide)
    sizes = (KERNEL_TAPS * narrow, wide, wide)
    spans = [round_up(o + n, 128) - o // 128 * 128 for o, n in zip(offsets, sizes)]
    width = round_up(offsets[2] + wide, 128)
    total = owners * groups
    steps = total.bit_length() - 1
    counts = chunk_rows(rows)
    outs = pl.pallas_call(
        functools.partial(gradient_kernel, owners, groups),
        out_shape=[
            jax.ShapeDtypeStruct((own_rows, channels), jnp.bfloat16),
            jax.ShapeDtypeStruct((wide, rows), jnp.float32),
            jax.ShapeDtypeStruct((KERNEL_TAPS, narrow, rows), jnp.float32),
            jax.ShapeDtypeStruct((wide, rows), jnp.float32),
        ],
        in_specs=[vmem] * 11,
        out_specs=[vmem] * 4,
        scratch_shapes=[pltpu.VMEM((total, n, width), jnp.bfloat16) for n in counts]
        + [pltpu.VMEM((total - 1, n, width), jnp.bfloat16) for n in counts]
        + [pltpu.VMEM((total - 1, n, width), jnp.bfloat16) for n in counts]
        + [pltpu.VMEM((owners, own_rows, n), jnp.bfloat16) for n in spans]
        + [pltpu.VMEM((inner, own_rows), jnp.bfloat16)] * 3
        + [pltpu.VMEM((own_rows, channels), jnp.float32)]
        + [pltpu.SemaphoreType.DMA((3, steps)), pltpu.SemaphoreType.DMA((3, steps))],
        compiler_params=pltpu.CompilerParams(
            collective_id=0, has_side_effects=True, vmem_limit_bytes=VMEM_LIMIT
        ),
        name="gradients",
    )(
        bucket_pos,
        bucket_len,
        mid_act,
        conv_cot,
        first_act,
        hidden_cot,
        upstream,
        out_act,
        weight_in,
        bucket,
        gain_in[None, :],
    )
    return (outs[0], outs[1], outs[2].transpose(1, 0, 2), outs[3])


def solution(mesh):
    return jax.shard_map(
        local,
        mesh=mesh,
        in_specs=(
            P(("dp", "shard"), None),
            P(),
            P(("dp", "shard")),
            P(("dp", "shard")),
            P(("dp", "shard")),
            P(("dp", "shard")),
            P(("dp", "shard")),
            P(("dp", "shard"), None),
            P(),
            P(),
            P(),
            P(),
            P(),
            P(),
        ),
        out_specs=(
            P(("dp", "shard"), None),
            P("dp", "shard"),
            P("dp", None, "shard"),
            P("dp", "shard"),
        ),
        check_vma=False,
    )
```
